32 devices in a mesh: row: 8 (over y, x, core), col: 4 (over z).
Axes of the slice: x: 2, y: 2, z: 4, core: 2. Of those that a mesh axis runs over, the one named last changes fastest.
Arguments:
- shear_stress: float32 [512, 16384], P(None, ('row', 'col')), may hold values from -3.5 to 3.5
- state_var: float32 [512, 16384], P(None, ('row', 'col')), may hold values from -0.4 to 0.4
- a_param: float32 [16384], P(('row', 'col')), may hold values from 0.7 to 1.4
- rate_param: float32 [16384], P(('row', 'col')), may hold values from 0.1 to 0.5
- loading: float32 [16384], P(('row', 'col')), may hold values from 0.1 to 1
- dense_tiles: bfloat16 [16384, 16384], P('row', 'col'), may hold values from -0.046875 to 0.046875
- left_factor: bfloat16 [512, 16384], P('col', 'row'), may hold values from -0.75 to 0.75
- right_factor: bfloat16 [512, 16384], P('row', 'col'), may hold values from -0.046875 to 0.046875
- admissible: int32 [8, 8], replicated, may hold values from 0 to 1, as said below
- tile_ranks: int32 [8, 8], replicated, may hold values from 16 to 64
Outputs:
- shear_next: float32 [512, 16384], P(None, ('row', 'col'))
- state_next: float32 [512, 16384], P(None, ('row', 'col'))
The draws below stay inside these ranges and needn't reach their ends.
Inputs may be any that keep to these rules, and one draw needn't show every extreme that they name: `admissible`: tiles on the diagonal and next to it are always dense; elsewhere a tile is dense or low-rank at random.
All inputs are finite; a program needn't handle non-finite values.
Results may differ from the reference program's by a relative error of at most 0.0024.
Values may be sent and summed in bfloat16 or wider, within the bound.
A program may use at most 128 MiB of HBM per device.

```python
import math
import jax
import jax.numpy as jnp
from jax import lax

TILE = 2048
RANK = 64
SCEN = 512
NB = 8
N = 16384


def draw_admissible(key, part):
    index_line = jnp.arange(NB, dtype=jnp.int32)
    nearby = jnp.abs(index_line[:, None] - index_line[None, :]) <= 1
    coins = jax.random.randint(key, (NB, NB), 0, 4) == 0
    return jnp.where(nearby | coins, 1, 0).astype(jnp.int32)


def touch_ends(array, key, smallest, largest):
    shape = array.shape
    index_at = [jax.random.randint(jax.random.fold_in(key, axis), (), 0, shape[axis]) for axis in range(len(shape))]
    array = array.at[tuple(index_at)].set(smallest)
    longest = shape.index(max(shape))
    index_at[longest] = (index_at[longest] + 1) % shape[longest]
    return array.at[tuple(index_at)].set(largest)


def steps_of(stream_key, dims, split, low, high):
    gain, own = 1.0, jax.random.fold_in(stream_key, 6)
    for position, blocks in split:
        heights = jnp.exp(jax.random.uniform(jax.random.fold_in(own, position), (blocks,), jnp.float32, low / len(split), high / len(split)))
        gain = gain * jnp.repeat(heights, dims[position] // blocks).reshape([-1 if axis == position else 1 for axis in range(len(dims))])
    return gain


def normal_values(key, extent, scale, bound, pieces=(), kind=jnp.bfloat16):
    array = scale * jax.random.normal(key, extent, jnp.float32)
    if pieces:
        array = array * steps_of(key, extent, pieces, -0.22, 0.18)
    return jnp.clip(array, -bound, bound).astype(kind)


def setup_inputs(seed: int = 0) -> dict:
    key_of = jax.random.split(jax.random.key(seed), 11)
    shear_stress = normal_values(key_of[0], (SCEN, N), 0.4, 3.5, ((1, 32),), jnp.float32)
    state_var = jnp.clip(jax.random.uniform(key_of[1], (SCEN, N), jnp.float32, -0.4, 0.4) * steps_of(key_of[1], (SCEN, N), ((1, 32),), -0.4, 0.0), -0.4, 0.4)
    a_param = jnp.clip(jnp.exp(math.log(1.4) - 0.6931472 * jax.random.uniform(key_of[2], (N,), jnp.float32) ** steps_of(key_of[2], (N,), ((0, 32),), -0.2, 0.2)), 0.7, 1.4)
    rate_param = jnp.clip(jnp.exp(math.log(0.5) - 1.609438 * jax.random.uniform(key_of[3], (N,), jnp.float32) ** steps_of(key_of[3], (N,), ((0, 32),), -0.2, 0.2)), 0.1, 0.5)
    loading = jnp.clip(jnp.exp(math.log(1.0) - 2.3025851 * jax.random.uniform(key_of[4], (N,), jnp.float32) ** steps_of(key_of[4], (N,), ((0, 32),), -0.2, 0.2)), 0.1, 1.0)
    dense_tiles = normal_values(key_of[5], (N, N), N ** -0.5, 0.046875, ((0, 8), (1, 4)))
    left_factor = normal_values(key_of[6], (NB * RANK, N), RANK ** -0.5, 0.75, ((0, 4), (1, 8)))
    right_factor = normal_values(key_of[7], (NB * RANK, N), N ** -0.5, 0.046875, ((0, 8), (1, 4)))
    admissible = draw_admissible(jax.random.fold_in(key_of[10], 71), 0)
    tile_ranks = touch_ends(jax.random.randint(key_of[9], (NB, NB), RANK // 4, RANK + 1), jax.random.fold_in(key_of[9], 1), RANK // 4, RANK).astype(jnp.int32)
    return dict(shear_stress=shear_stress, state_var=state_var, a_param=a_param, rate_param=rate_param, loading=loading, dense_tiles=dense_tiles, left_factor=left_factor, right_factor=right_factor, admissible=admissible, tile_ranks=tile_ranks)


def slip_velocity(shear_now, state_now, a_param):
    return jnp.sinh(shear_now / a_param[None, :]) * jnp.exp(-state_now)


def tile_product(vec_tile, dense_tile, left_tile, right_tile, is_dense, rank_here):
    def dense_branch(operands):
        return lax.dot_general(operands[0], operands[1], (((1,), (1,)), ((), ())), preferred_element_type=jnp.float32)

    def factor_branch(operands):
        projection = lax.dot_general(operands[0], operands[3], (((1,), (1,)), ((), ())), preferred_element_type=jnp.float32)
        keep_mask = jnp.arange(projection.shape[1], dtype=jnp.int32)[None, :] < rank_here
        projection = jnp.where(keep_mask, projection, jnp.zeros_like(projection)).astype(jnp.bfloat16)
        return jnp.dot(projection, operands[2], preferred_element_type=jnp.float32)

    return lax.cond(is_dense == 1, dense_branch, factor_branch, (vec_tile, dense_tile, left_tile, right_tile))


def interaction(rounded, dense_tiles, left_factor, right_factor, admissible, tile_ranks):
    def target_row(row_tile):
        def source_col(accum_sum, col_tile):
            vec_tile = lax.dynamic_slice_in_dim(rounded, col_tile * TILE, TILE, 1)
            dense_tile = lax.dynamic_slice(dense_tiles, (row_tile * TILE, col_tile * TILE), (TILE, TILE))
            left_tile = lax.dynamic_slice(left_factor, (col_tile * RANK, row_tile * TILE), (RANK, TILE))
            right_tile = lax.dynamic_slice(right_factor, (row_tile * RANK, col_tile * TILE), (RANK, TILE))
            term = tile_product(vec_tile, dense_tile, left_tile, right_tile, admissible[row_tile, col_tile], tile_ranks[row_tile, col_tile])
            return accum_sum + term, None

        accum_sum, unused_out = lax.scan(source_col, jnp.zeros((SCEN, TILE), jnp.float32), jnp.arange(NB, dtype=jnp.int32))
        return accum_sum

    blocks = lax.map(target_row, jnp.arange(NB, dtype=jnp.int32))
    return jnp.transpose(blocks, (1, 0, 2)).reshape(SCEN, N)


def reference(shear_stress, state_var, a_param, rate_param, loading, dense_tiles, left_factor, right_factor, admissible, tile_ranks):
    def rates(shear_now, state_now):
        velocity = slip_velocity(shear_now, state_now, a_param)
        rounded = velocity.astype(jnp.bfloat16)
        pushed = interaction(rounded, dense_tiles, left_factor, right_factor, admissible, tile_ranks)
        k_shear = loading[None, :] - pushed
        k_state = rate_param[None, :] * (jnp.exp(-state_now) - jnp.abs(velocity))
        return k_shear, k_state

    k_shear1, k_state1 = rates(shear_stress, state_var)
    shear_mid = shear_stress + 0.5 * k_shear1
    state_mid = state_var + 0.5 * k_state1
    k_shear2, k_state2 = rates(shear_mid, state_mid)
    shear_next = shear_stress + 0.25 * (k_shear1 + k_shear2)
    state_next = state_var + 0.25 * (k_state1 + k_state2)
    return (shear_next, state_next)
```

```python
import functools
import math

import jax
import jax.numpy as jnp
from jax import lax
from jax.experimental import pallas as pl
from jax.experimental.pallas import tpu as pltpu
from jax.sharding import PartitionSpec as P

TILE = 2048
RANK = 64
GROUP = 16
LAG = 4
LN2 = math.log(2.0)
MESH = pl.DeviceIdType.MESH
F32 = jnp.float32
BF16 = jnp.bfloat16


def kernel(
    rows,
    cols,
    shear_ref,
    state_ref,
    a_ref,
    rate_ref,
    load_ref,
    dense_ref,
    left_ref,
    right_ref,
    adm_ref,
    rank_ref,
    shear_out,
    state_out,
    weights,
    gathered,
    vsend,
    psend,
    precv,
    own,
    k_shear,
    k_state,
    masked,
    dense_sem,
    p1_send,
    p1_recv,
    p2_send,
    fwd_send,
    p2_recv,
    rs_send,
    rs_recv,
):
    scenarios, piece = shear_ref.shape
    chunk = rows * GROUP
    chunks = scenarios // chunk
    gap = max(0, LAG - chunks)
    half = rows // 2
    per = rows // cols
    r = lax.axis_index("row")
    c = lax.axis_index("col")
    block = r // per
    slot = (r % per) * cols + c
    sib = r + 1 - 2 * (r % 2)
    targets, sources = weights.shape
    across = sources // TILE
    down = targets // TILE

    dense_copy = pltpu.make_async_copy(dense_ref, weights, dense_sem)

    def scen(q):
        return pl.ds(pl.multiple_of(q * chunk, chunk), chunk)

    def group_of(u, g):
        return gathered.at[u, pl.ds(pl.multiple_of(g * GROUP, GROUP), GROUP), :]

    def p1_copy(u, j):
        return pltpu.make_async_remote_copy(
            src_ref=vsend.at[u, pl.ds(pl.multiple_of(j * GROUP, GROUP), GROUP), :],
            dst_ref=gathered.at[
                u,
                pl.ds(pl.multiple_of(j * GROUP, GROUP), GROUP),
                pl.ds(pl.multiple_of(slot * piece, piece), piece),
            ],
            send_sem=p1_send.at[u, j],
            recv_sem=p1_recv.at[u],
            device_id=(j, block),
            device_id_type=MESH,
        )

    def p1_here(u, j):
        return pltpu.make_async_copy(
            vsend.at[u, pl.ds(pl.multiple_of(j * GROUP, GROUP), GROUP), :],
            gathered.at[
                u,
                pl.ds(pl.multiple_of(j * GROUP, GROUP), GROUP),
                pl.ds(pl.multiple_of(slot * piece, piece), piece),
            ],
            p1_recv.at[u],
        )

    def group_copy(u, g, send_sem, row_to):
        return pltpu.make_async_remote_copy(
            src_ref=group_of(u, g),
            dst_ref=group_of(u, g),
            send_sem=send_sem,
            recv_sem=p2_recv.at[u, g],
            device_id=(row_to, c),
            device_id_type=MESH,
        )

    def rs_copy(u, z):
        return pltpu.make_async_remote_copy(
            src_ref=psend.at[u, z],
            dst_ref=precv.at[u, c],
            send_sem=rs_send.at[u, z],
            recv_sem=rs_recv.at[u, c],
            device_id=(r, z),
            device_id_type=MESH,
        )

    def rs_arrival(u, z):
        return pltpu.make_async_remote_copy(
            src_ref=psend.at[u, z],
            dst_ref=precv.at[u, z],
            send_sem=rs_send.at[u, z],
            recv_sem=rs_recv.at[u, z],
            device_id=(r, z),
            device_id_type=MESH,
        )

    def velocity(shear_now, state_now):
        x = shear_now / a_ref[...]
        fade = jnp.exp(-state_now)
        v = (jnp.exp(x - LN2) - jnp.exp(-x - LN2)) * fade
        return v, rate_ref[...] * (fade - jnp.abs(v))

    def send_slip(u):
        def one(i, _):
            j = (r + 1 + i) % rows
            here = (j == r) & (block == c)

            @pl.when(here)
            def _():
                p1_here(u, j).start()

            @pl.when(jnp.logical_not(here))
            def _():
                p1_copy(u, j).start()

            return 0

        lax.fori_loop(0, rows, one, 0)

    def first_slip(q, _):
        v, ks = velocity(shear_ref[scen(q), :], state_ref[scen(q), :])
        vsend[q] = v.astype(BF16)
        k_state[scen(q), :] = ks
        send_slip(q)
        return 0

    def spread(u):
        pltpu.make_async_copy(group_of(u, r), group_of(u, r), p1_recv.at[u]).wait()
        group_copy(u, r, p2_send.at[u, half - 1], sib).start()

        def one(i, _):
            group_copy(u, r, p2_send.at[u, i], (r + 2 * (i + 1)) % rows).start()
            return 0

        lax.fori_loop(0, half - 1, one, 0)

    def forward(u):
        def one(i, _):
            g = (r + 2 * (i + 1)) % rows
            group_copy(u, g, fwd_send.at[u, i], sib).wait_recv()
            group_copy(u, g, fwd_send.at[u, i], sib).start()
            return 0

        lax.fori_loop(0, half - 1, one, 0)

    def multiply(u):
        def arrive(i, _):
            group_copy(u, (sib + 2 * i) % rows, p1_send.at[u, 0], sib).wait_recv()
            return 0

        lax.fori_loop(0, half, arrive, 0)

        def one(i, _):
            z = (c + 1 + i) % cols
            part = lax.dot_general(
                gathered[u],
                weights[pl.ds(pl.multiple_of(z * piece, piece), piece), :],
                (((1,), (1,)), ((), ())),
                preferred_element_type=F32,
            )

            @pl.when(i < cols - 1)
            def _():
                psend[u, z] = part.astype(BF16)
                rs_copy(u, z).start()

            @pl.when(i == cols - 1)
            def _():
                own[u] = part

            return 0

        lax.fori_loop(0, cols, one, 0)

    def finish(u):
        def one(i, _):
            z = (c + 1 + i) % cols
            rs_arrival(u, z).wait_recv()
            own[u] = own[u] + precv[u, z].astype(F32)
            return 0

        lax.fori_loop(0, cols - 1, one, 0)

        @pl.when(u < chunks)
        def _():
            here = scen(u)
            ks = load_ref[...] - own[u]
            k_shear[here, :] = ks
            k1 = k_state[here, :]
            state = state_ref[here, :]
            v, k2 = velocity(shear_ref[here, :] + 0.5 * ks, state + 0.5 * k1)
            vsend[u + chunks] = v.astype(BF16)
            send_slip(u + chunks)
            state_out[here, :] = state + 0.25 * (k1 + k2)

        @pl.when(u >= chunks)
        def _():
            here = scen(u - chunks)
            ks = load_ref[...] - own[u]
            shear_out[here, :] = shear_ref[here, :] + 0.25 * (k_shear[here, :] + ks)

    build_rows = 256
    builds = targets // build_rows
    build_cols = 512

    def build(b, _):
        start = pl.multiple_of(b * build_rows, build_rows)
        here = pl.ds(start, build_rows)
        td = (b * build_rows) // TILE
        for k in range(across):
            dense = adm_ref[r * down + td, c * across + k]
            rank = rank_ref[r * down + td, c * across + k]
            left = left_ref[k * RANK : (k + 1) * RANK, here]
            keep = lax.broadcasted_iota(jnp.int32, (RANK, build_rows), 0) < rank
            left = jnp.where(keep, left.astype(F32), 0.0)
            left = jnp.transpose(left).astype(BF16)
            for s in range(TILE // build_cols):
                span = slice(k * TILE + s * build_cols, k * TILE + (s + 1) * build_cols)
                right = right_ref[pl.ds(pl.multiple_of(td * RANK, RANK), RANK), span]
                term = jnp.dot(left, right, preferred_element_type=F32)
                is_dense = jnp.full(term.shape, dense, jnp.int32) == 1
                weights[here, span] = jnp.where(
                    is_dense, weights[here, span].astype(F32), term
                ).astype(BF16)
        return 0

    dense_copy.start()
    lax.fori_loop(0, chunks, first_slip, 0)

    def at_slot(sigma, body):
        valid = ((sigma >= 0) & (sigma < chunks)) | (
            (sigma >= chunks + gap) & (sigma < 2 * chunks + gap)
        )
        u = jnp.where(sigma < chunks, sigma, sigma - gap)

        @pl.when(valid)
        def _():
            body(u)

    def step(t, _):
        at_slot(t, spread)
        at_slot(t - 1, forward)

        @pl.when(t == 0)
        def _():
            dense_copy.wait()

        @pl.when(t < 2)
        def _():
            lax.fori_loop(t * builds // 2, (t + 1) * builds // 2, build, 0)

        at_slot(t - 2, multiply)
        at_slot(t - 3, finish)
        return 0

    lax.fori_loop(0, 2 * chunks + gap + 3, step, 0)

    def drain(u, _):
        def p1(j, _):
            @pl.when(jnp.logical_not((j == r) & (block == c)))
            def _():
                p1_copy(u, j).wait_send()

            return 0

        lax.fori_loop(0, rows, p1, 0)

        def p2(i, _):
            group_copy(u, r, p2_send.at[u, i], sib).wait_send()
            return 0

        lax.fori_loop(0, half, p2, 0)

        def fwd(i, _):
            group_copy(u, r, fwd_send.at[u, i], sib).wait_send()
            return 0

        lax.fori_loop(0, half - 1, fwd, 0)

        def rs(i, _):
            rs_copy(u, (c + 1 + i) % cols).wait_send()
            return 0

        lax.fori_loop(0, cols - 1, rs, 0)
        return 0

    lax.fori_loop(0, 2 * chunks, drain, 0)


def solution(mesh):
    rows, cols = mesh.shape["row"], mesh.shape["col"]

    def on_device(
        shear, state, a_param, rate, loading, dense, left, right, admissible, ranks
    ):
        scenarios, piece = shear.shape
        chunk = rows * GROUP
        units = 2 * (scenarios // chunk)
        vmem = pl.BlockSpec(memory_space=pltpu.VMEM)
        smem = pl.BlockSpec(memory_space=pltpu.SMEM)
        hbm = pl.BlockSpec(memory_space=pl.ANY)
        dma = pltpu.SemaphoreType.DMA
        return pl.pallas_call(
            functools.partial(kernel, rows, cols),
            out_shape=(
                jax.ShapeDtypeStruct(shear.shape, F32),
                jax.ShapeDtypeStruct(shear.shape, F32),
            ),
            in_specs=[vmem] * 5 + [hbm, vmem, vmem, smem, smem],
            out_specs=(vmem, vmem),
            scratch_shapes=[
                pltpu.VMEM(dense.shape, BF16),
                pltpu.VMEM((units, chunk, dense.shape[1]), BF16),
                pltpu.VMEM((units, chunk, piece), BF16),
                pltpu.VMEM((units, cols, chunk, piece), BF16),
                pltpu.VMEM((units, cols, chunk, piece), BF16),
                pltpu.VMEM((units, chunk, piece), F32),
                pltpu.VMEM(shear.shape, F32),
                pltpu.VMEM(shear.shape, F32),
                pltpu.VMEM((8, 128), F32),
                dma,
                dma((units, rows)),
                dma((units,)),
                dma((units, rows // 2)),
                dma((units, rows // 2)),
                dma((units, rows)),
                dma((units, cols)),
                dma((units, cols)),
            ],
            compiler_params=pltpu.CompilerParams(
                has_side_effects=True, vmem_limit_bytes=62 * 1024 * 1024
            ),
        )(
            shear,
            state,
            a_param[None, :],
            rate[None, :],
            loading[None, :],
            dense,
            left,
            right,
            admissible,
            ranks,
        )

    wide = P(None, ("row", "col"))
    line = P(("row", "col"))
    placed = (
        wide,
        wide,
        line,
        line,
        line,
        P("row", "col"),
        P("col", "row"),
        P("row", "col"),
        P(),
        P(),
    )
    return jax.shard_map(
        on_device, mesh=mesh, in_specs=placed, out_specs=(wide, wide), check_vma=False
    )
```

```python
import functools
import math

import jax
import jax.numpy as jnp
from jax import lax
from jax.experimental import pallas as pl
from jax.experimental.pallas import tpu as pltpu
from jax.sharding import PartitionSpec as P

TILE = 2048
RANK = 64
GROUP = 16
LAG = 4
LN2 = math.log(2.0)
MESH = pl.DeviceIdType.MESH
F32 = jnp.float32
BF16 = jnp.bfloat16


def kernel(
    rows,
    cols,
    shear_ref,
    state_ref,
    a_ref,
    rate_ref,
    load_ref,
    dense_ref,
    left_ref,
    right_ref,
    adm_ref,
    rank_ref,
    shear_out,
    state_out,
    weights,
    gathered,
    vsend,
    staged,
    psend,
    precv,
    own,
    k_shear,
    k_state,
    dense_sem,
    st_send,
    st_recv,
    p1_send,
    p1_recv,
    p2_send,
    fwd_send,
    p2_recv,
    rs_send,
    rs_recv,
):
    scenarios, piece = shear_ref.shape
    chunk = rows * GROUP
    chunks = scenarios // chunk
    gap = max(0, LAG - chunks)
    half = rows // 2
    per = rows // cols
    r = lax.axis_index("row")
    c = lax.axis_index("col")
    mine = c * per
    sib = r + 1 - 2 * (r % 2)
    targets, sources = weights.shape
    across = sources // TILE
    down = targets // TILE

    dense_copy = pltpu.make_async_copy(dense_ref, weights, dense_sem)

    def scen(q):
        return pl.ds(pl.multiple_of(q * chunk, chunk), chunk)

    def group_of(u, g):
        return gathered.at[u, pl.ds(pl.multiple_of(g * GROUP, GROUP), GROUP), :]

    def part_of(u, g):
        return vsend.at[u, pl.ds(pl.multiple_of(g * GROUP, GROUP), GROUP), :]

    def st_copy(u, j):
        return pltpu.make_async_remote_copy(
            src_ref=part_of(u, j),
            dst_ref=staged.at[u, r],
            send_sem=st_send.at[u, j],
            recv_sem=st_recv.at[u],
            device_id=(j, c),
            device_id_type=MESH,
        )

    def place(u, source):
        slot = (source % per) * cols + c
        return gathered.at[
            u,
            pl.ds(pl.multiple_of(r * GROUP, GROUP), GROUP),
            pl.ds(pl.multiple_of(slot * piece, piece), piece),
        ]

    def p1_copy(u, source):
        return pltpu.make_async_remote_copy(
            src_ref=staged.at[u, source],
            dst_ref=place(u, source),
            send_sem=p1_send.at[u, source],
            recv_sem=p1_recv.at[u],
            device_id=(r, source // per),
            device_id_type=MESH,
        )

    def group_copy(u, g, send_sem, row_to):
        return pltpu.make_async_remote_copy(
            src_ref=group_of(u, g),
            dst_ref=group_of(u, g),
            send_sem=send_sem,
            recv_sem=p2_recv.at[u, g],
            device_id=(row_to, c),
            device_id_type=MESH,
        )

    def rs_copy(u, z):
        return pltpu.make_async_remote_copy(
            src_ref=psend.at[u, z],
            dst_ref=precv.at[u, c],
            send_sem=rs_send.at[u, z],
            recv_sem=rs_recv.at[u, c],
            device_id=(r, z),
            device_id_type=MESH,
        )

    def rs_arrival(u, z):
        return pltpu.make_async_remote_copy(
            src_ref=psend.at[u, z],
            dst_ref=precv.at[u, z],
            send_sem=rs_send.at[u, z],
            recv_sem=rs_recv.at[u, z],
            device_id=(r, z),
            device_id_type=MESH,
        )

    def velocity(shear_now, state_now):
        x = shear_now / a_ref[...]
        fade = jnp.exp(-state_now)
        v = (jnp.exp(x - LN2) - jnp.exp(-x - LN2)) * fade
        return v, rate_ref[...] * (fade - jnp.abs(v))

    def send_slip(u):
        def one(i, _):
            st_copy(u, (r + 1 + i) % rows).start()
            return 0

        lax.fori_loop(0, rows - 1, one, 0)
        pltpu.make_async_copy(part_of(u, r), staged.at[u, r], st_recv.at[u]).start()

    def relay(u):
        pltpu.make_async_copy(staged.at[u], staged.at[u], st_recv.at[u]).wait()

        def one(i, _):
            p1_copy(u, (mine + per + i) % rows).start()
            return 0

        lax.fori_loop(0, rows - per, one, 0)

        def stay(i, _):
            pltpu.make_async_copy(
                staged.at[u, mine + i], place(u, mine + i), p1_recv.at[u]
            ).start()
            return 0

        lax.fori_loop(0, per, stay, 0)

    def first_slip(q, _):
        v, ks = velocity(shear_ref[scen(q), :], state_ref[scen(q), :])
        vsend[q] = v.astype(BF16)
        k_state[scen(q), :] = ks
        send_slip(q)
        return 0

    def spread(u):
        pltpu.make_async_copy(group_of(u, r), group_of(u, r), p1_recv.at[u]).wait()
        group_copy(u, r, p2_send.at[u, half - 1], sib).start()

        def one(i, _):
            group_copy(u, r, p2_send.at[u, i], (r + 2 * (i + 1)) % rows).start()
            return 0

        lax.fori_loop(0, half - 1, one, 0)

    def forward(u):
        def one(i, _):
            g = (r + 2 * (i + 1)) % rows
            group_copy(u, g, fwd_send.at[u, i], sib).wait_recv()
            group_copy(u, g, fwd_send.at[u, i], sib).start()
            return 0

        lax.fori_loop(0, half - 1, one, 0)

    def multiply(u):
        def arrive(i, _):
            group_copy(u, (sib + 2 * i) % rows, p1_send.at[u, 0], sib).wait_recv()
            return 0

        lax.fori_loop(0, half, arrive, 0)

        def one(i, _):
            z = (c + 1 + i) % cols
            part = lax.dot_general(
                gathered[u],
                weights[pl.ds(pl.multiple_of(z * piece, piece), piece), :],
                (((1,), (1,)), ((), ())),
                preferred_element_type=F32,
            )

            @pl.when(i < cols - 1)
            def _():
                psend[u, z] = part.astype(BF16)
                rs_copy(u, z).start()

            @pl.when(i == cols - 1)
            def _():
                own[u] = part

            return 0

        lax.fori_loop(0, cols, one, 0)

    def finish(u):
        def one(i, _):
            z = (c + 1 + i) % cols
            rs_arrival(u, z).wait_recv()
            own[u] = own[u] + precv[u, z].astype(F32)
            return 0

        lax.fori_loop(0, cols - 1, one, 0)

        @pl.when(u < chunks)
        def _():
            here = scen(u)
            ks = load_ref[...] - own[u]
            k_shear[here, :] = ks
            k1 = k_state[here, :]
            state = state_ref[here, :]
            v, k2 = velocity(shear_ref[here, :] + 0.5 * ks, state + 0.5 * k1)
            vsend[u + chunks] = v.astype(BF16)
            send_slip(u + chunks)
            state_out[here, :] = state + 0.25 * (k1 + k2)

        @pl.when(u >= chunks)
        def _():
            here = scen(u - chunks)
            ks = load_ref[...] - own[u]
            shear_out[here, :] = shear_ref[here, :] + 0.25 * (k_shear[here, :] + ks)

    build_rows = 256
    builds = targets // build_rows
    build_cols = 512

    def build(b, _):
        start = pl.multiple_of(b * build_rows, build_rows)
        here = pl.ds(start, build_rows)
        td = (b * build_rows) // TILE
        for k in range(across):
            dense = adm_ref[r * down + td, c * across + k]
            rank = rank_ref[r * down + td, c * across + k]
            left = left_ref[k * RANK : (k + 1) * RANK, here]
            keep = lax.broadcasted_iota(jnp.int32, (RANK, build_rows), 0) < rank
            left = jnp.where(keep, left.astype(F32), 0.0)
            left = jnp.transpose(left).astype(BF16)
            for s in range(TILE // build_cols):
                span = slice(k * TILE + s * build_cols, k * TILE + (s + 1) * build_cols)
                right = right_ref[pl.ds(pl.multiple_of(td * RANK, RANK), RANK), span]
                term = jnp.dot(left, right, preferred_element_type=F32)
                is_dense = jnp.full(term.shape, dense, jnp.int32) == 1
                weights[here, span] = jnp.where(
                    is_dense, weights[here, span].astype(F32), term
                ).astype(BF16)
        return 0

    dense_copy.start()
    lax.fori_loop(0, chunks, first_slip, 0)

    def at_slot(sigma, body):
        valid = ((sigma >= 0) & (sigma < chunks)) | (
            (sigma >= chunks + gap) & (sigma < 2 * chunks + gap)
        )
        u = jnp.where(sigma < chunks, sigma, sigma - gap)

        @pl.when(valid)
        def _():
            body(u)

    def step(t, _):
        at_slot(t - 1, forward)
        at_slot(t, relay)
        at_slot(t - 2, multiply)
        at_slot(t, spread)

        @pl.when(t == 0)
        def _():
            dense_copy.wait()

        @pl.when(t < 2)
        def _():
            lax.fori_loop(t * builds // 2, (t + 1) * builds // 2, build, 0)

        at_slot(t - 3, finish)
        return 0

    lax.fori_loop(0, 2 * chunks + gap + 3, step, 0)

    def drain(u, _):
        def st(i, _):
            st_copy(u, (r + 1 + i) % rows).wait_send()
            return 0

        lax.fori_loop(0, rows - 1, st, 0)

        def p1(i, _):
            p1_copy(u, (mine + per + i) % rows).wait_send()
            return 0

        lax.fori_loop(0, rows - per, p1, 0)

        def p2(i, _):
            group_copy(u, r, p2_send.at[u, i], sib).wait_send()
            return 0

        lax.fori_loop(0, half, p2, 0)

        def fwd(i, _):
            group_copy(u, r, fwd_send.at[u, i], sib).wait_send()
            return 0

        lax.fori_loop(0, half - 1, fwd, 0)

        def rs(i, _):
            rs_copy(u, (c + 1 + i) % cols).wait_send()
            return 0

        lax.fori_loop(0, cols - 1, rs, 0)
        return 0

    lax.fori_loop(0, 2 * chunks, drain, 0)


def solution(mesh):
    rows, cols = mesh.shape["row"], mesh.shape["col"]

    def on_device(
        shear, state, a_param, rate, loading, dense, left, right, admissible, ranks
    ):
        scenarios, piece = shear.shape
        chunk = rows * GROUP
        units = 2 * (scenarios // chunk)
        vmem = pl.BlockSpec(memory_space=pltpu.VMEM)
        smem = pl.BlockSpec(memory_space=pltpu.SMEM)
        hbm = pl.BlockSpec(memory_space=pl.ANY)
        dma = pltpu.SemaphoreType.DMA
        return pl.pallas_call(
            functools.partial(kernel, rows, cols),
            out_shape=(
                jax.ShapeDtypeStruct(shear.shape, F32),
                jax.ShapeDtypeStruct(shear.shape, F32),
            ),
            in_specs=[vmem] * 5 + [hbm, vmem, vmem, smem, smem],
            out_specs=(vmem, vmem),
            scratch_shapes=[
                pltpu.VMEM(dense.shape, BF16),
                pltpu.VMEM((units, chunk, dense.shape[1]), BF16),
                pltpu.VMEM((units, chunk, piece), BF16),
                pltpu.VMEM((units, rows, GROUP, piece), BF16),
                pltpu.VMEM((units, cols, chunk, piece), BF16),
                pltpu.VMEM((units, cols, chunk, piece), BF16),
                pltpu.VMEM((units, chunk, piece), F32),
                pltpu.VMEM(shear.shape, F32),
                pltpu.VMEM(shear.shape, F32),
                dma,
                dma((units, rows)),
                dma((units,)),
                dma((units, rows)),
                dma((units,)),
                dma((units, rows // 2)),
                dma((units, rows // 2)),
                dma((units, rows)),
                dma((units, cols)),
                dma((units, cols)),
            ],
            compiler_params=pltpu.CompilerParams(
                has_side_effects=True, vmem_limit_bytes=62 * 1024 * 1024
            ),
        )(
            shear,
            state,
            a_param[None, :],
            rate[None, :],
            loading[None, :],
            dense,
            left,
            right,
            admissible,
            ranks,
        )

    wide = P(None, ("row", "col"))
    line = P(("row", "col"))
    placed = (
        wide,
        wide,
        line,
        line,
        line,
        P("row", "col"),
        P("col", "row"),
        P("row", "col"),
        P(),
        P(),
    )
    return jax.shard_map(
        on_device, mesh=mesh, in_specs=placed, out_specs=(wide, wide), check_vma=False
    )
```

```python
import functools
import math

import jax
import jax.numpy as jnp
from jax import lax
from jax.experimental import pallas as pl
from jax.experimental.pallas import tpu as pltpu
from jax.sharding import PartitionSpec as P

TILE = 2048
RANK = 64
GROUP = 16
LAG = 4
LN2 = math.log(2.0)
MESH = pl.DeviceIdType.MESH
F32 = jnp.float32
BF16 = jnp.bfloat16


def kernel(
    rows,
    cols,
    shear_ref,
    state_ref,
    a_ref,
    rate_ref,
    load_ref,
    dense_ref,
    left_ref,
    right_ref,
    adm_ref,
    rank_ref,
    shear_out,
    state_out,
    weights,
    gathered,
    vsend,
    staged,
    psend,
    precv,
    own,
    k_shear,
    k_state,
    dense_sem,
    st_send,
    st_recv,
    p1_send,
    p1_recv,
    p2_send,
    fwd_send,
    p2_recv,
    rs_send,
    rs_recv,
):
    scenarios, piece = shear_ref.shape
    chunk = rows * GROUP
    chunks = scenarios // chunk
    gap = max(0, LAG - chunks)
    half = rows // 2
    per = rows // cols
    r = lax.axis_index("row")
    c = lax.axis_index("col")
    mine = c * per
    sib = r + 1 - 2 * (r % 2)
    targets, sources = weights.shape
    across = sources // TILE
    down = targets // TILE

    dense_copy = pltpu.make_async_copy(dense_ref, weights, dense_sem)

    def scen(q):
        return pl.ds(pl.multiple_of(q * chunk, chunk), chunk)

    def group_of(u, g):
        return gathered.at[u, pl.ds(pl.multiple_of(g * GROUP, GROUP), GROUP), :]

    def part_of(u, g):
        return vsend.at[u, pl.ds(pl.multiple_of(g * GROUP, GROUP), GROUP), :]

    def st_copy(u, j):
        return pltpu.make_async_remote_copy(
            src_ref=part_of(u, j),
            dst_ref=staged.at[u, r],
            send_sem=st_send.at[u, j],
            recv_sem=st_recv.at[u],
            device_id=(j, c),
            device_id_type=MESH,
        )

    def place(u, source):
        slot = (source % per) * cols + c
        return gathered.at[
            u,
            pl.ds(pl.multiple_of(r * GROUP, GROUP), GROUP),
            pl.ds(pl.multiple_of(slot * piece, piece), piece),
        ]

    def p1_copy(u, source):
        return pltpu.make_async_remote_copy(
            src_ref=staged.at[u, source],
            dst_ref=place(u, source),
            send_sem=p1_send.at[u, source],
            recv_sem=p1_recv.at[u],
            device_id=(r, source // per),
            device_id_type=MESH,
        )

    def group_copy(u, g, send_sem, row_to):
        return pltpu.make_async_remote_copy(
            src_ref=group_of(u, g),
            dst_ref=group_of(u, g),
            send_sem=send_sem,
            recv_sem=p2_recv.at[u, g],
            device_id=(row_to, c),
            device_id_type=MESH,
        )

    def rs_copy(u, z):
        return pltpu.make_async_remote_copy(
            src_ref=psend.at[u, z],
            dst_ref=precv.at[u, c],
            send_sem=rs_send.at[u, z],
            recv_sem=rs_recv.at[u, c],
            device_id=(r, z),
            device_id_type=MESH,
        )

    def rs_arrival(u, z):
        return pltpu.make_async_remote_copy(
            src_ref=psend.at[u, z],
            dst_ref=precv.at[u, z],
            send_sem=rs_send.at[u, z],
            recv_sem=rs_recv.at[u, z],
            device_id=(r, z),
            device_id_type=MESH,
        )

    def velocity(shear_now, state_now):
        x = shear_now / a_ref[...]
        fade = jnp.exp(-state_now)
        v = (jnp.exp(x - LN2) - jnp.exp(-x - LN2)) * fade
        return v, rate_ref[...] * (fade - jnp.abs(v))

    def send_slip(u):
        def one(i, _):
            st_copy(u, (r + 1 + i) % rows).start()
            return 0

        lax.fori_loop(0, rows - 1, one, 0)
        pltpu.make_async_copy(part_of(u, r), staged.at[u, r], st_recv.at[u]).start()

    def relay(u):
        pltpu.make_async_copy(staged.at[u], staged.at[u], st_recv.at[u]).wait()

        def one(i, _):
            p1_copy(u, (mine + per + i) % rows).start()
            return 0

        lax.fori_loop(0, rows - per, one, 0)

        def stay(i, _):
            pltpu.make_async_copy(
                staged.at[u, mine + i], place(u, mine + i), p1_recv.at[u]
            ).start()
            return 0

        lax.fori_loop(0, per, stay, 0)

    def first_slip(q, _):
        v, ks = velocity(shear_ref[scen(q), :], state_ref[scen(q), :])
        vsend[q] = v.astype(BF16)
        k_state[scen(q), :] = ks
        send_slip(q)
        return 0

    def spread(u):
        pltpu.make_async_copy(group_of(u, r), group_of(u, r), p1_recv.at[u]).wait()
        group_copy(u, r, p2_send.at[u, half - 1], sib).start()

        def one(i, _):
            group_copy(u, r, p2_send.at[u, i], (r + 2 * (i + 1)) % rows).start()
            return 0

        lax.fori_loop(0, half - 1, one, 0)

    def forward(u):
        def one(i, _):
            g = (r + 2 * (i + 1)) % rows
            group_copy(u, g, fwd_send.at[u, i], sib).wait_recv()
            group_copy(u, g, fwd_send.at[u, i], sib).start()
            return 0

        lax.fori_loop(0, half - 1, one, 0)

    def multiply(u):
        def arrive(i, _):
            group_copy(u, (sib + 2 * i) % rows, p1_send.at[u, 0], sib).wait_recv()
            return 0

        lax.fori_loop(0, half, arrive, 0)

        def one(i, _):
            z = (c + 1 + i) % cols
            part = lax.dot_general(
                gathered[u],
                weights[pl.ds(pl.multiple_of(z * piece, piece), piece), :],
                (((1,), (1,)), ((), ())),
                preferred_element_type=F32,
            )

            @pl.when(i < cols - 1)
            def _():
                psend[u, z] = part.astype(BF16)
                rs_copy(u, z).start()

            @pl.when(i == cols - 1)
            def _():
                own[u] = part

            return 0

        lax.fori_loop(0, cols, one, 0)

    def finish(u):
        def one(i, _):
            z = (c + 1 + i) % cols
            rs_arrival(u, z).wait_recv()
            own[u] = own[u] + precv[u, z].astype(F32)
            return 0

        lax.fori_loop(0, cols - 1, one, 0)

        @pl.when(u < chunks)
        def _():
            here = scen(u)
            ks = load_ref[...] - own[u]
            k_shear[here, :] = ks
            k1 = k_state[here, :]
            state = state_ref[here, :]
            v, k2 = velocity(shear_ref[here, :] + 0.5 * ks, state + 0.5 * k1)
            vsend[u + chunks] = v.astype(BF16)
            send_slip(u + chunks)
            state_out[here, :] = state + 0.25 * (k1 + k2)

        @pl.when(u >= chunks)
        def _():
            here = scen(u - chunks)
            ks = load_ref[...] - own[u]
            shear_out[here, :] = shear_ref[here, :] + 0.25 * (k_shear[here, :] + ks)

    build_rows = 256
    builds = targets // build_rows
    build_cols = 512

    def build(b, _):
        start = pl.multiple_of(b * build_rows, build_rows)
        here = pl.ds(start, build_rows)
        td = (b * build_rows) // TILE
        for k in range(across):
            dense = adm_ref[r * down + td, c * across + k]
            rank = rank_ref[r * down + td, c * across + k]
            left = left_ref[k * RANK : (k + 1) * RANK, here]
            keep = lax.broadcasted_iota(jnp.int32, (RANK, build_rows), 0) < rank
            left = jnp.where(keep, left.astype(F32), 0.0)
            left = jnp.transpose(left).astype(BF16)
            for s in range(TILE // build_cols):
                span = slice(k * TILE + s * build_cols, k * TILE + (s + 1) * build_cols)
                right = right_ref[pl.ds(pl.multiple_of(td * RANK, RANK), RANK), span]
                term = jnp.dot(left, right, preferred_element_type=F32)
                is_dense = jnp.full(term.shape, dense, jnp.int32) == 1
                weights[here, span] = jnp.where(
                    is_dense, weights[here, span].astype(F32), term
                ).astype(BF16)
        return 0

    dense_copy.start()
    lax.fori_loop(0, chunks, first_slip, 0)

    def first_relay(q, _):
        relay(q)
        return 0

    lax.fori_loop(0, chunks, first_relay, 0)

    def at_slot(sigma, body):
        valid = ((sigma >= 0) & (sigma < chunks)) | (
            (sigma >= chunks + gap) & (sigma < 2 * chunks + gap)
        )
        u = jnp.where(sigma < chunks, sigma, sigma - gap)

        @pl.when(valid)
        def _():
            body(u)

    def step(t, _):
        at_slot(t - 2, multiply)

        @pl.when((t >= chunks + gap) & (t < 2 * chunks + gap))
        def _():
            relay(t - gap)

        at_slot(t - 1, forward)
        at_slot(t, spread)

        @pl.when(t == 0)
        def _():
            dense_copy.wait()

        @pl.when(t < 2)
        def _():
            lax.fori_loop(t * builds // 2, (t + 1) * builds // 2, build, 0)

        at_slot(t - 3, finish)
        return 0

    lax.fori_loop(0, 2 * chunks + gap + 3, step, 0)

    def drain(u, _):
        def st(i, _):
            st_copy(u, (r + 1 + i) % rows).wait_send()
            return 0

        lax.fori_loop(0, rows - 1, st, 0)

        def p1(i, _):
            p1_copy(u, (mine + per + i) % rows).wait_send()
            return 0

        lax.fori_loop(0, rows - per, p1, 0)

        def p2(i, _):
            group_copy(u, r, p2_send.at[u, i], sib).wait_send()
            return 0

        lax.fori_loop(0, half, p2, 0)

        def fwd(i, _):
            group_copy(u, r, fwd_send.at[u, i], sib).wait_send()
            return 0

        lax.fori_loop(0, half - 1, fwd, 0)

        def rs(i, _):
            rs_copy(u, (c + 1 + i) % cols).wait_send()
            return 0

        lax.fori_loop(0, cols - 1, rs, 0)
        return 0

    lax.fori_loop(0, 2 * chunks, drain, 0)


def solution(mesh):
    rows, cols = mesh.shape["row"], mesh.shape["col"]

    def on_device(
        shear, state, a_param, rate, loading, dense, left, right, admissible, ranks
    ):
        scenarios, piece = shear.shape
        chunk = rows * GROUP
        units = 2 * (scenarios // chunk)
        vmem = pl.BlockSpec(memory_space=pltpu.VMEM)
        smem = pl.BlockSpec(memory_space=pltpu.SMEM)
        hbm = pl.BlockSpec(memory_space=pl.ANY)
        dma = pltpu.SemaphoreType.DMA
        return pl.pallas_call(
            functools.partial(kernel, rows, cols),
            out_shape=(
                jax.ShapeDtypeStruct(shear.shape, F32),
                jax.ShapeDtypeStruct(shear.shape, F32),
            ),
            in_specs=[vmem] * 5 + [hbm, vmem, vmem, smem, smem],
            out_specs=(vmem, vmem),
            scratch_shapes=[
                pltpu.VMEM(dense.shape, BF16),
                pltpu.VMEM((units, chunk, dense.shape[1]), BF16),
                pltpu.VMEM((units, chunk, piece), BF16),
                pltpu.VMEM((units, rows, GROUP, piece), BF16),
                pltpu.VMEM((units, cols, chunk, piece), BF16),
                pltpu.VMEM((units, cols, chunk, piece), BF16),
                pltpu.VMEM((units, chunk, piece), F32),
                pltpu.VMEM(shear.shape, F32),
                pltpu.VMEM(shear.shape, F32),
                dma,
                dma((units, rows)),
                dma((units,)),
                dma((units, rows)),
                dma((units,)),
                dma((units, rows // 2)),
                dma((units, rows // 2)),
                dma((units, rows)),
                dma((units, cols)),
                dma((units, cols)),
            ],
            compiler_params=pltpu.CompilerParams(
                has_side_effects=True, vmem_limit_bytes=62 * 1024 * 1024
            ),
        )(
            shear,
            state,
            a_param[None, :],
            rate[None, :],
            loading[None, :],
            dense,
            left,
            right,
            admissible,
            ranks,
        )

    wide = P(None, ("row", "col"))
    line = P(("row", "col"))
    placed = (
        wide,
        wide,
        line,
        line,
        line,
        P("row", "col"),
        P("col", "row"),
        P("row", "col"),
        P(),
        P(),
    )
    return jax.shard_map(
        on_device, mesh=mesh, in_specs=placed, out_specs=(wide, wide), check_vma=False
    )
```
